256 devices in a mesh: dp: 16 (over y_lo, z), lat: 16 (over y_hi, x, core).
Axes of the slice: x: 4, y: 4 (y_hi: 2, y_lo: 2; y = y_hi * 2 + y_lo), z: 8, core: 2. Of those that a mesh axis runs over, the one named last changes fastest.
Arguments:
- tokens: bfloat16 [4096, 8192], P('dp', 'lat'), may hold values from -6 to 6
- enc_weight: bfloat16 [8192, 4096], P(None, 'lat'), may hold values from -0.0625 to 0.0625
- enc_bias: float32 [4096], P('lat'), may hold values from -3 to 3
- dec_weight: bfloat16 [4096, 8192], P('lat'), may hold values from -0.25 to 0.25
- dec_bias: bfloat16 [8192], P('lat'), may hold values from -3 to 3
- block_ids: int32 [16, 8], P('dp'), may hold values from 0 to 31, as said below
- counts: int32 [16], P('dp'), may hold values from 4 to 8
Outputs:
- error: bfloat16 [4096, 8192], P('dp', 'lat')
- grad_enc: float32 [8192, 4096], P('dp', 'lat')
- grad_dec: float32 [4096, 8192], P('lat', 'dp')
The draws below stay inside these ranges and needn't reach their ends.
Inputs may be any that keep to these rules, and one draw needn't show every extreme that they name: `block_ids`: in each row the 8 entries are different latent block numbers; entries past the row's count are not used.
All inputs are finite; a program needn't handle non-finite values.
Results may differ from the reference program's by a relative error of at most 0.015.
Values may be sent and summed in bfloat16 or wider, within the bound.
No kernel may reach another device: no remote copies, remote signals or barrier semaphores. Data moves between devices by JAX's collectives and lax.ppermute only.
A program may use at most 128 MiB of HBM per device.

```python
import math
import jax
import jax.numpy as jnp
from jax import lax

D = 8192
BLK = 128
TBLK = 256
SLOTS = 8
NBLK_DEV = 2
NBLOCKS = 32
LAT = 4096
TOKENS = 4096
TBLOCKS = 16
N_LAT = 16


def draw_block_ids(key, part):
    base_score = jax.random.randint(key, (TBLOCKS, NBLOCKS), 0, 4 * NBLOCKS)
    heat_level = jax.random.randint(jax.random.fold_in(key, 7), (NBLOCKS,), 0, 3) * (2 * NBLOCKS)
    score = (base_score + heat_level[None, :]) * NBLOCKS + jnp.arange(NBLOCKS, dtype=jnp.int32)[None, :]
    picked = lax.top_k(score, SLOTS)[1]
    return picked.astype(jnp.int32)


def draw_counts(key, part):
    values = jax.random.randint(key, (TBLOCKS,), SLOTS // 2, SLOTS + 1)
    position = jax.random.randint(jax.random.fold_in(key, 3), (), 0, TBLOCKS)
    values = values.at[position].set(SLOTS)
    return values.astype(jnp.int32)


def steps_of(key, dims, split, low, top_value):
    factor_of = 1.0
    for axis_at, blocks in split:
        steps = jax.random.uniform(jax.random.fold_in(jax.random.fold_in(key, 6), axis_at), (blocks,), jnp.float32, low / len(split), top_value / len(split))
        factor_of = factor_of * jnp.repeat(jnp.exp(steps), dims[axis_at] // blocks).reshape((-1,) + (1,) * (len(dims) - 1 - axis_at))
    return factor_of


def scatter_about(own_key, shape, deviation, most, cuts=(), kind=jnp.bfloat16):
    values = deviation * jax.random.normal(own_key, shape, jnp.float32)
    if cuts:
        values = values * steps_of(own_key, shape, cuts, -0.22, 0.18)
    return jnp.clip(values, -most, most).astype(kind)


def setup_inputs(seed: int = 0) -> dict:
    splits = jax.random.split(jax.random.key(seed), 8)
    tokens = scatter_about(splits[0], (TOKENS, D), 1.0, 6.0, ((0, 16), (1, 16)))
    enc_weight = scatter_about(splits[1], (D, LAT), D ** -0.5, 0.0625, ((1, 16),))
    enc_bias = scatter_about(splits[2], (LAT,), 0.5, 3.0, ((0, 16),), jnp.float32)
    dec_weight = scatter_about(splits[3], (LAT, D), (SLOTS * BLK // 2) ** -0.5, 0.25, ((0, 16),))
    dec_bias = scatter_about(splits[4], (D,), 0.5, 3.0, ((0, 16),))
    block_ids = draw_block_ids(jax.random.fold_in(splits[7], 71), 0)
    counts = draw_counts(jax.random.fold_in(splits[7], 71), 0)
    return {"tokens": tokens, "enc_weight": enc_weight, "enc_bias": enc_bias, "dec_weight": dec_weight, "dec_bias": dec_bias, "block_ids": block_ids, "counts": counts}


def reference(tokens, enc_weight, enc_bias, dec_weight, dec_bias, block_ids, counts):
    token_blocks = tokens.reshape(TOKENS // TBLK, TBLK, D)
    scale_factor = 1.0 / math.sqrt(TOKENS)
    owner_ids = jnp.arange(N_LAT, dtype=jnp.int32)

    def one_block(carry, inputs):
        enc_grad, dec_grad = carry
        block_tokens, id_row, count_now = inputs
        act_list = []
        pre_list = []
        contrib_list = []
        for slot in range(SLOTS):
            col_start = (id_row[slot] * BLK).astype(jnp.int32)
            valid = jnp.where(slot < count_now, 1.0, 0.0).astype(jnp.float32)
            weight_cols = lax.dynamic_slice_in_dim(enc_weight, col_start, BLK, 1)
            bias_cols = lax.dynamic_slice_in_dim(enc_bias, col_start, BLK, 0)
            weight_rows = lax.dynamic_slice_in_dim(dec_weight, col_start, BLK, 0)
            preact = jnp.dot(block_tokens, weight_cols, preferred_element_type=jnp.float32) + bias_cols
            activations = (jnp.maximum(preact, 0.0) * valid).astype(jnp.bfloat16)
            act_list.append(activations)
            pre_list.append(jnp.where(valid > 0, preact, -1.0))
            contrib_list.append(jnp.dot(activations, weight_rows, preferred_element_type=jnp.float32))
        contribs = jnp.stack(contrib_list, 0)
        owners = (id_row // NBLK_DEV).astype(jnp.int32)
        one_hot = (owners[:, None] == owner_ids[None, :]).astype(jnp.float32)
        partials = jnp.einsum('ko,ktd->otd', one_hot, contribs, precision=lax.Precision.HIGHEST).astype(jnp.bfloat16)
        recon = lax.optimization_barrier(jnp.sum(partials.astype(jnp.float32), axis=0)) + dec_bias.astype(jnp.float32)
        error = (recon - block_tokens.astype(jnp.float32)).astype(jnp.bfloat16)
        for slot in range(SLOTS):
            col_start = (id_row[slot] * BLK).astype(jnp.int32)
            weight_rows = lax.dynamic_slice_in_dim(dec_weight, col_start, BLK, 0)
            grad_full = lax.dot_general(error, weight_rows, (((1,), (1,)), ((), ())), preferred_element_type=jnp.float32)
            gated = jnp.where(pre_list[slot] > 0, grad_full, 0.0).astype(jnp.bfloat16)
            enc_term = lax.dot_general(block_tokens, gated, (((0,), (0,)), ((), ())), preferred_element_type=jnp.float32)
            dec_term = lax.dot_general(act_list[slot], error, (((0,), (0,)), ((), ())), preferred_element_type=jnp.float32)
            zero_index = jnp.zeros((), jnp.int32)
            old_enc = lax.dynamic_slice(enc_grad, (zero_index, col_start), (D, BLK))
            enc_grad = lax.dynamic_update_slice(enc_grad, old_enc + enc_term, (zero_index, col_start))
            old_dec = lax.dynamic_slice(dec_grad, (col_start, zero_index), (BLK, D))
            dec_grad = lax.dynamic_update_slice(dec_grad, old_dec + dec_term, (col_start, zero_index))
        return ((enc_grad, dec_grad), error)
    start_carry = (jnp.zeros((D, LAT), jnp.float32), jnp.zeros((LAT, D), jnp.float32))
    (enc_grad, dec_grad), errors = lax.scan(one_block, start_carry, (token_blocks, block_ids, counts))
    return (errors.reshape(TOKENS, D), enc_grad * scale_factor, dec_grad * scale_factor)
```

```python
import math

import jax
import jax.numpy as jnp
from jax import lax
from jax.experimental import pallas as pl
from jax.experimental.pallas import tpu as pltpu
from jax.sharding import PartitionSpec as P

BLK = 128
F32 = jnp.float32
BF16 = jnp.bfloat16


def exchange(x, axis):
    return lax.all_to_all(x, axis, 0, 0, tiled=False)


def split3(x):
    hi = lax.reduce_precision(x, 8, 7)
    rest = x - hi
    mid = lax.reduce_precision(rest, 8, 7)
    return hi, mid, rest - mid


def pick_body(ids_ref, table_ref, out_ref):
    groups, rows, _ = out_ref.shape
    slots = ids_ref.shape[1]
    sub = rows // (2 * slots)

    def step(t, carry):
        for k in range(slots):
            block = ids_ref[t, k]
            for w in range(2):
                src = pl.multiple_of((w * 2 + block % 2) * sub, sub)
                out_ref[t, pl.ds((w * slots + k) * sub, sub), :] = table_ref[block // 2, pl.ds(src, sub), :]
        return carry

    lax.fori_loop(0, groups, step, 0)


def pick(ids, table, sub):
    groups, slots = ids.shape
    return pl.pallas_call(
        pick_body,
        out_shape=jax.ShapeDtypeStruct((groups, 2 * slots * sub, BLK), BF16),
        in_specs=[pl.BlockSpec(memory_space=pltpu.SMEM), pl.BlockSpec(memory_space=pltpu.VMEM)],
        out_specs=pl.BlockSpec(memory_space=pltpu.VMEM),
        name="pick",
    )(ids, table)


def gather_sum_body(ids_ref, parts_ref, out_ref, acc_ref):
    groups, rows, _ = parts_ref.shape
    slots = ids_ref.shape[1]
    sub = rows // (2 * slots)
    acc_ref[...] = jnp.zeros_like(acc_ref)

    def step(t, carry):
        for k in range(slots):
            block = ids_ref[t, k]
            for w in range(2):
                part = parts_ref[t, pl.ds((w * slots + k) * sub, sub), :].astype(F32)
                acc_ref[block, pl.ds(w * sub, sub), :] += part
        return carry

    lax.fori_loop(0, groups, step, 0)
    out_ref[...] = acc_ref[...].astype(BF16)


def gather_sum(ids, parts, blocks):
    slots = ids.shape[1]
    sub = parts.shape[1] // (2 * slots)
    return pl.pallas_call(
        gather_sum_body,
        out_shape=jax.ShapeDtypeStruct((blocks, 2 * sub, BLK), BF16),
        in_specs=[pl.BlockSpec(memory_space=pltpu.SMEM), pl.BlockSpec(memory_space=pltpu.VMEM)],
        out_specs=pl.BlockSpec(memory_space=pltpu.VMEM),
        scratch_shapes=[pltpu.VMEM((blocks, 2 * sub, BLK), F32)],
        name="gather_sum",
    )(ids, parts)


def local(tokens, enc_weight, enc_bias, dec_weight, dec_bias, block_ids, counts):
    n_dp, n_lat = lax.axis_size("dp"), lax.axis_size("lat")
    d, t = lax.axis_index("dp"), lax.axis_index("lat")
    token_count, width = tokens.shape
    owned = enc_weight.shape[1] // BLK
    blocks = owned * n_lat
    slots = block_ids.shape[1]
    sub = width // n_lat
    flip = [(i * n_lat + j, j * n_dp + i) for i in range(n_dp) for j in range(n_lat)]

    bias_rows = jnp.broadcast_to(dec_bias[None, :], (16, width))
    moved = lax.ppermute(jnp.concatenate([tokens, bias_rows], axis=0), ("dp", "lat"), flip)
    tok, out_bias = moved[:token_count], moved[token_count : token_count + 1]

    listed = jnp.concatenate([block_ids, counts[:, None]], axis=1)
    listed = jnp.pad(listed, ((0, 0), (0, BLK - slots - 1)))
    lists = exchange(jnp.broadcast_to(listed[None], (n_dp, 1, BLK)), "dp")[:, 0, :]
    ids = jnp.clip(lists[:, :slots], 0, blocks - 1)
    my_list = lax.dynamic_slice_in_dim(lists, t, 1, 0)
    my_ids = jnp.clip(my_list[0, :slots], 0, blocks - 1)
    live = jnp.arange(slots) < my_list[0, slots]
    live_row = jnp.repeat(live, BLK)[None, :]

    enc_part = lax.dynamic_slice_in_dim(enc_weight, d * width, width, 0)
    dec_part = lax.dynamic_slice_in_dim(dec_weight, d * width, width, 1).T
    spread = jnp.stack([enc_part, dec_part]).reshape(2, n_lat, sub, owned, BLK)
    spread = spread.transpose(1, 0, 3, 2, 4).reshape(n_lat, 2 * owned * sub, BLK)
    bias_parts = jnp.stack(split3(enc_bias.reshape(owned, BLK))).reshape(3 * owned, BLK)
    bias_parts = jnp.pad(bias_parts, ((0, 8 - 3 * owned), (0, 0))).astype(BF16)
    spread = jnp.concatenate([spread, jnp.broadcast_to(bias_parts[None], (n_lat, 8, BLK))], axis=1)
    table = exchange(spread, "lat")
    all_bias = table[:, 2 * owned * sub :, :].astype(F32)
    all_bias = all_bias[:, :owned] + all_bias[:, owned : 2 * owned] + all_bias[:, 2 * owned : 3 * owned]
    my_bias = all_bias.reshape(blocks, BLK)[my_ids].reshape(1, slots * BLK)
    picked = exchange(pick(ids, table, sub), "lat")
    picked = picked.reshape(n_lat, 2, slots, sub, BLK).transpose(1, 0, 3, 2, 4)
    picked = picked.reshape(2, width, slots * BLK)
    enc_sel, dec_sel = picked[0], picked[1]

    share = token_count // n_dp
    partial = jnp.dot(tok, enc_sel, preferred_element_type=F32)
    preact = jnp.sum(exchange(partial.reshape(n_dp, share, slots * BLK), "dp"), axis=0) + my_bias
    act_share = jnp.where(live_row, jnp.maximum(preact, 0.0), 0.0)
    gate = act_share > 0
    act_share = act_share.astype(BF16)
    acts = exchange(jnp.broadcast_to(act_share[None], (n_dp, share, slots * BLK)), "dp")
    acts = acts.reshape(token_count, slots * BLK)

    recon = lax.dot_general(acts, dec_sel, (((1,), (1,)), ((), ())), preferred_element_type=F32)
    error = (recon + out_bias.astype(F32) - tok.astype(F32)).astype(BF16)
    error_out = lax.ppermute(error, ("dp", "lat"), [(b, a) for a, b in flip])

    back = jnp.dot(error, dec_sel, preferred_element_type=F32).astype(BF16)
    back = jnp.sum(exchange(back.reshape(n_dp, share, slots * BLK), "dp").astype(F32), axis=0)
    back = jnp.where(gate, back, 0.0).astype(BF16)
    gated = exchange(jnp.broadcast_to(back[None], (n_dp, share, slots * BLK)), "dp")
    gated = gated.reshape(token_count, slots * BLK)

    over_tokens = (((0,), (0,)), ((), ()))
    dec_grad = lax.dot_general(error, acts, over_tokens, preferred_element_type=F32).astype(BF16)
    enc_grad = lax.dot_general(tok, gated, over_tokens, preferred_element_type=F32).astype(BF16)
    grads = jnp.stack([enc_grad, dec_grad]).reshape(2, n_lat, sub, slots, BLK)
    grads = grads.transpose(1, 0, 3, 2, 4).reshape(n_lat, 2 * slots * sub, BLK)
    summed = gather_sum(ids, exchange(grads, "lat"), blocks)
    done = exchange(summed.reshape(n_lat, owned * 2 * sub, BLK), "lat")
    done = done.reshape(n_lat, owned, 2, sub, BLK).astype(F32) * (1.0 / math.sqrt(token_count * n_dp))
    enc_out = done[:, :, 0].transpose(0, 2, 1, 3).reshape(width, owned * BLK)
    dec_out = done[:, :, 1].transpose(1, 3, 0, 2).reshape(owned * BLK, width)
    return error_out, enc_out, dec_out


def solution(mesh):
    placed = (
        P("dp", "lat"),
        P(None, "lat"),
        P("lat"),
        P("lat", None),
        P("lat"),
        P("dp", None),
        P("dp"),
    )
    return jax.shard_map(
        local,
        mesh=mesh,
        in_specs=placed,
        out_specs=(P("dp", "lat"), P("dp", "lat"), P("lat", "dp")),
        check_vma=False,
    )
```

```python
import math

import jax
import jax.numpy as jnp
from jax import lax
from jax.experimental import pallas as pl
from jax.experimental.pallas import tpu as pltpu
from jax.sharding import PartitionSpec as P


BLK = 128
F32 = jnp.float32
BF16 = jnp.bfloat16


def exchange(x, axis):
    return lax.all_to_all(x, axis, 0, 0, tiled=False)


def split3(x):
    hi = lax.reduce_precision(x, 8, 7)
    rest = x - hi
    mid = lax.reduce_precision(rest, 8, 7)
    return hi, mid, rest - mid


def pick_body(ids_ref, table_ref, out_ref):
    groups, rows, _ = out_ref.shape
    slots = ids_ref.shape[1]
    sub = rows // (2 * slots)

    def step(t, carry):
        for k in range(slots):
            block = ids_ref[t, k]
            for w in range(2):
                src = pl.multiple_of((w * 2 + block % 2) * sub, sub)
                out_ref[t, pl.ds((w * slots + k) * sub, sub), :] = table_ref[block // 2, pl.ds(src, sub), :]
        return carry

    lax.fori_loop(0, groups, step, 0)


def pick(ids, table, sub):
    groups, slots = ids.shape
    return pl.pallas_call(
        pick_body,
        out_shape=jax.ShapeDtypeStruct((groups, 2 * slots * sub, BLK), BF16),
        in_specs=[pl.BlockSpec(memory_space=pltpu.SMEM), pl.BlockSpec(memory_space=pltpu.VMEM)],
        out_specs=pl.BlockSpec(memory_space=pltpu.VMEM),
        name="pick",
    )(ids, table)


def gather_sum_body(ids_ref, parts_ref, out_ref, acc_ref):
    groups, rows, _ = parts_ref.shape
    slots = ids_ref.shape[1]
    sub = rows // (2 * slots)
    acc_ref[...] = jnp.zeros_like(acc_ref)

    def step(t, carry):
        for k in range(slots):
            block = ids_ref[t, k]
            for w in range(2):
                part = parts_ref[t, pl.ds((w * slots + k) * sub, sub), :].astype(F32)
                acc_ref[block, pl.ds(w * sub, sub), :] += part
        return carry

    lax.fori_loop(0, groups, step, 0)
    out_ref[...] = acc_ref[...].astype(BF16)


def gather_sum(ids, parts, blocks):
    slots = ids.shape[1]
    sub = parts.shape[1] // (2 * slots)
    return pl.pallas_call(
        gather_sum_body,
        out_shape=jax.ShapeDtypeStruct((blocks, 2 * sub, BLK), BF16),
        in_specs=[pl.BlockSpec(memory_space=pltpu.SMEM), pl.BlockSpec(memory_space=pltpu.VMEM)],
        out_specs=pl.BlockSpec(memory_space=pltpu.VMEM),
        scratch_shapes=[pltpu.VMEM((blocks, 2 * sub, BLK), F32)],
        name="gather_sum",
    )(ids, parts)


def spread_rows(parts, groups):
    weights, width, cols = parts.shape
    sub = width // groups
    rows = parts.reshape(weights, groups, sub, cols // BLK, BLK).transpose(1, 0, 3, 2, 4)
    return rows.reshape(groups, weights * (cols // BLK) * sub, BLK)


def local(tokens, enc_weight, enc_bias, dec_weight, dec_bias, block_ids, counts):
    n_dp, n_lat = lax.axis_size("dp"), lax.axis_size("lat")
    d = lax.axis_index("dp")
    token_count, width = tokens.shape
    owned = enc_weight.shape[1] // BLK
    blocks = owned * n_lat
    slots = block_ids.shape[1]
    sub = width // n_lat
    flip = [(i * n_lat + j, j * n_dp + i) for i in range(n_dp) for j in range(n_lat)]

    listed = jnp.concatenate([block_ids, counts[:, None]], axis=1).astype(BF16)
    listed = jnp.pad(listed, ((0, 0), (0, BLK - slots - 1)))
    listed = lax.ppermute(listed, ("dp", "lat"), flip)

    bias_rows = jnp.broadcast_to(dec_bias[None, :], (16, width))
    moved = lax.ppermute(jnp.concatenate([tokens, bias_rows], axis=0), ("dp", "lat"), flip)
    tok, out_bias = moved[:token_count], moved[token_count : token_count + 1]

    enc_part = lax.dynamic_slice_in_dim(enc_weight, d * width, width, 0)
    dec_part = lax.dynamic_slice_in_dim(dec_weight, d * width, width, 1).T
    spread = spread_rows(jnp.stack([enc_part, dec_part]), n_lat)
    main = spread.shape[1]
    extra = [p.reshape(owned, BLK).astype(BF16) for p in split3(enc_bias)] + [listed]
    extra = jnp.concatenate(extra, axis=0)
    extra = jnp.pad(extra, ((0, -extra.shape[0] % 8), (0, 0)))
    spread = jnp.concatenate([spread, jnp.broadcast_to(extra[None], (n_lat,) + extra.shape)], axis=1)
    table = exchange(spread, "lat")
    extra = table[:, main:].astype(F32)
    lists = extra[:, 3 * owned].astype(jnp.int32)
    ids = jnp.clip(lists[:, :slots], 0, blocks - 1)
    picked = pick(ids, table, sub)
    picked = exchange(picked, "lat")
    my_list = listed[0].astype(F32).astype(jnp.int32)
    live_row = jnp.repeat(jnp.arange(slots) < my_list[slots], BLK)[None, :]
    all_bias = extra[:, :owned] + extra[:, owned : 2 * owned] + extra[:, 2 * owned : 3 * owned]
    my_ids = jnp.clip(my_list[:slots], 0, blocks - 1)
    my_bias = all_bias.reshape(blocks, BLK)[my_ids].reshape(1, slots * BLK)
    picked = picked.reshape(n_lat, 2, slots, sub, BLK).transpose(1, 0, 3, 2, 4)
    picked = picked.reshape(2, width, slots * BLK)
    enc_sel, dec_sel = picked[0], picked[1]

    share = token_count // n_dp
    partial = jnp.dot(tok, enc_sel, preferred_element_type=F32).reshape(n_dp, share, slots * BLK)
    partial = exchange(partial, "dp")
    preact = jnp.sum(partial, axis=0) + my_bias
    act_share = jnp.where(live_row, jnp.maximum(preact, 0.0), 0.0)
    gate = act_share > 0
    act_share = act_share.astype(BF16)
    acts = exchange(jnp.broadcast_to(act_share[None], (n_dp, share, slots * BLK)), "dp")
    acts = acts.reshape(token_count, slots * BLK)

    recon = lax.dot_general(acts, dec_sel, (((1,), (1,)), ((), ())), preferred_element_type=F32)
    error = (recon + out_bias.astype(F32) - tok.astype(F32)).astype(BF16)
    back = jnp.dot(error, dec_sel, preferred_element_type=F32).astype(BF16)
    back = exchange(back.reshape(n_dp, share, slots * BLK), "dp")
    error_out = lax.ppermute(error, ("dp", "lat"), [(b, a) for a, b in flip])
    back = jnp.where(gate, jnp.sum(back.astype(F32), axis=0), 0.0).astype(BF16)
    gated = exchange(jnp.broadcast_to(back[None], (n_dp, share, slots * BLK)), "dp")
    gated = gated.reshape(token_count, slots * BLK)

    over_tokens = (((0,), (0,)), ((), ()))
    scale = 1.0 / math.sqrt(token_count * n_dp)
    dec_grad = lax.dot_general(error, acts, over_tokens, preferred_element_type=F32).astype(BF16)
    enc_grad = lax.dot_general(tok, gated, over_tokens, preferred_element_type=F32).astype(BF16)
    parts = spread_rows(jnp.stack([enc_grad, dec_grad]), n_lat)
    parts = exchange(parts, "lat")
    total = gather_sum(ids, parts, blocks).reshape(n_lat, owned * 2 * sub, BLK)
    total = exchange(total, "lat")
    total = total.reshape(n_lat, owned, 2, sub, BLK).astype(F32) * scale
    enc_out = total[:, :, 0].transpose(0, 2, 1, 3).reshape(width, owned * BLK)
    dec_out = total[:, :, 1].transpose(1, 3, 0, 2).reshape(owned * BLK, width)
    return error_out, enc_out, dec_out


def solution(mesh):
    placed = (
        P("dp", "lat"),
        P(None, "lat"),
        P("lat"),
        P("lat", None),
        P("lat"),
        P("dp", None),
        P("dp"),
    )
    return jax.shard_map(
        local,
        mesh=mesh,
        in_specs=placed,
        out_specs=(P("dp", "lat"), P("dp", "lat"), P("lat", "dp")),
        check_vma=False,
    )
```
